32 devices in a mesh: segment: 8 (over z, x), tp: 4 (over y, core).
Axes of the slice: x: 2, y: 2, z: 4, core: 2. Of those that a mesh axis runs over, the one named last changes fastest.
Arguments:
- layer_inputs: bfloat16 [8, 2, 128, 2048], P('segment', None, 'tp'), may hold values from -100 to 100, as said below
- cotangent: bfloat16 [2, 2, 128, 2048], P(None, None, 'tp'), may hold values from -6 to 6
- gate_weight: bfloat16 [8, 2048, 4096], P('segment', None, 'tp'), may hold values from -1 to 1, as said below
- up_weight: bfloat16 [8, 2048, 4096], P('segment', None, 'tp'), may hold values from -1 to 1, as said below
- down_weight: bfloat16 [8, 4096, 2048], P('segment', 'tp'), may hold values from -1 to 1, as said below
- gate_momentum: float32 [8, 1024, 4096], P('segment', None, 'tp'), may hold values from -48 to 48
- up_momentum: float32 [8, 1024, 4096], P('segment', None, 'tp'), may hold values from -48 to 48
- down_momentum: float32 [8, 4096, 1024], P('segment', 'tp'), may hold values from -48 to 48
Outputs:
- input_gradient: bfloat16 [8, 2, 128, 2048], P('segment', None, 'tp')
- new_gate_momentum: float32 [8, 1024, 4096], P('segment', None, 'tp')
- new_up_momentum: float32 [8, 1024, 4096], P('segment', None, 'tp')
- new_down_momentum: float32 [8, 4096, 1024], P('segment', 'tp')
The draws below stay inside these ranges and needn't reach their ends.
Inputs may be any that keep to these rules, and one draw needn't show every extreme that they name: `layer_inputs`: stored layer inputs, independent for every section and micro-batch. `gate_weight`: sections 2l and 2l + 1 hold equal copies of one layer's weights. `up_weight`: sections 2l and 2l + 1 hold equal copies of one layer's weights. `down_weight`: sections 2l and 2l + 1 hold equal copies of one layer's weights.
All inputs are finite; a program needn't handle non-finite values.
Results may differ from the reference program's by a relative error of at most 0.02.
Values may be sent and summed in bfloat16 or wider, within the bound.
A program may use at most 128 MiB of HBM per device.

```python
import math
import jax
import jax.numpy as jnp
from jax import lax

D = 2048
FF = 4096
ROWS = 128
MICRO = 2
LAYERS = 4
HALF = 1024
FF_DEV = 1024
N_TP = 4


def clipped_normal(key, shape):
    return jnp.clip(jax.random.normal(key, shape, jnp.float32), -4.0, 4.0)


def draw_layer_inputs(key, part):
    shape = (2 * LAYERS, MICRO, ROWS, D)
    noise_key, row_key, column_key = jax.random.split(jax.random.fold_in(key, 101), 3)
    noise = clipped_normal(noise_key, shape)
    row_scale = jnp.exp(jax.random.uniform(row_key, (2 * LAYERS, MICRO, ROWS, 1), jnp.float32, 0.0, math.log(10.0)))
    column_scale = jnp.exp(jax.random.uniform(column_key, (2 * LAYERS, MICRO, 1, D), jnp.float32, math.log(0.25), math.log(2.5)))
    return (noise * row_scale * column_scale).astype(jnp.bfloat16)


def mirrored(key, shape, fan_in):
    values = clipped_normal(key, shape)
    values = values * fan_in ** (-0.5)
    return jnp.repeat(values, 2, axis=0).astype(jnp.bfloat16)


def draw_gate_weight(key, part):
    return mirrored(jax.random.fold_in(key, 211), (LAYERS, D, FF), D)


def draw_up_weight(key, part):
    return mirrored(jax.random.fold_in(key, 223), (LAYERS, D, FF), D)


def draw_down_weight(key, part):
    return mirrored(jax.random.fold_in(key, 227), (LAYERS, FF, D), FF)


def block_levels(key, extent, cuts, low, largest):
    def one(dim, shards_of):
        steps = jax.random.uniform(jax.random.fold_in(jax.random.fold_in(key, 6), dim), (shards_of,), jnp.float32, low / len(cuts), largest / len(cuts))
        return jnp.repeat(jnp.exp(steps), extent[dim] // shards_of).reshape((-1,) + (1,) * (len(extent) - dim - 1))

    loudness = one(*cuts[0])
    for cut in cuts[1:]:
        loudness = loudness * one(*cut)
    return loudness


def centred(stream_key, extent, deviation, most, cuts=(), held_as=jnp.bfloat16):
    entries = deviation * jax.random.normal(stream_key, extent, jnp.float32)
    if cuts:
        entries = entries * block_levels(stream_key, extent, cuts, -0.22, 0.18)
    return jnp.clip(entries, -most, most).astype(held_as)


def setup_inputs(seed: int = 0) -> dict:
    key_list = jax.random.split(jax.random.key(seed), 9)
    layer_inputs = draw_layer_inputs(jax.random.fold_in(key_list[8], 71), 0)
    cotangent = centred(key_list[1], (2, MICRO, ROWS, D), 1.0, 6.0, ((2, 4),))
    gate_weight = draw_gate_weight(jax.random.fold_in(key_list[8], 71), 0)
    up_weight = draw_up_weight(jax.random.fold_in(key_list[8], 71), 0)
    down_weight = draw_down_weight(jax.random.fold_in(key_list[8], 71), 0)
    gate_momentum = centred(key_list[5], (2 * LAYERS, HALF, FF), 8.0, 48.0, ((0, 8), (2, 4)), jnp.float32)
    up_momentum = centred(key_list[6], (2 * LAYERS, HALF, FF), 8.0, 48.0, ((0, 8), (2, 4)), jnp.float32)
    down_momentum = centred(key_list[7], (2 * LAYERS, FF, HALF), 8.0, 48.0, ((0, 8), (1, 4)), jnp.float32)
    return dict(layer_inputs=layer_inputs, cotangent=cotangent, gate_weight=gate_weight, up_weight=up_weight, down_weight=down_weight, gate_momentum=gate_momentum, up_momentum=up_momentum, down_momentum=down_momentum)


epsilon = 1e-05
momentum_decay = 0.9

def rounded(values):
    return lax.optimization_barrier(values.astype(jnp.bfloat16)).astype(jnp.float32)

def section_backward(inputs, incoming, gate_weight, up_weight, down_weight):
    rows = inputs.reshape(-1, D).astype(jnp.float32)
    inverse_norm = lax.rsqrt(lax.optimization_barrier(jnp.mean(rows * rows, axis=-1, keepdims=True)) + epsilon)
    exact = rows * inverse_norm
    normed = exact.astype(jnp.bfloat16)
    gate = jnp.dot(normed, gate_weight, preferred_element_type=jnp.float32)
    up = jnp.dot(normed, up_weight, preferred_element_type=jnp.float32)
    sigma = jax.nn.sigmoid(gate)
    silu = gate * sigma
    hidden = (silu * up).astype(jnp.bfloat16)
    arriving = incoming.reshape(-1, D)
    hidden_grad = jnp.dot(arriving, down_weight.T, preferred_element_type=jnp.float32)
    gate_grad = (hidden_grad * up * sigma * (1.0 + gate * (1.0 - sigma))).astype(jnp.bfloat16)
    up_grad = (hidden_grad * silu).astype(jnp.bfloat16)
    gate_parts = jnp.einsum('rgf,dgf->grd', gate_grad.astype(jnp.float32).reshape(-1, N_TP, FF_DEV), gate_weight.astype(jnp.float32).reshape(D, N_TP, FF_DEV), precision=lax.Precision.HIGHEST)
    up_parts = jnp.einsum('rgf,dgf->grd', up_grad.astype(jnp.float32).reshape(-1, N_TP, FF_DEV), up_weight.astype(jnp.float32).reshape(D, N_TP, FF_DEV), precision=lax.Precision.HIGHEST)
    parts = lax.optimization_barrier((gate_parts + up_parts).astype(jnp.bfloat16))
    normed_grad = lax.optimization_barrier(jnp.sum(parts.astype(jnp.float32), axis=0))
    back = arriving.astype(jnp.float32) + inverse_norm * (normed_grad - exact * lax.optimization_barrier(jnp.mean(normed_grad * exact, axis=-1, keepdims=True)))
    back = back.astype(jnp.bfloat16).reshape(inputs.shape)
    weights = (jnp.dot(normed.T, gate_grad, preferred_element_type=jnp.float32), jnp.dot(normed.T, up_grad, preferred_element_type=jnp.float32), jnp.dot(hidden.T, arriving, preferred_element_type=jnp.float32))
    return (back, weights)

def reference(layer_inputs, cotangent, gate_weight, up_weight, down_weight, gate_momentum, up_momentum, down_momentum):

    def step(incoming, position):
        sections = (2 * position, 2 * position + 1)
        backs = []
        totals = []
        for direction in range(2):
            section = sections[direction]
            back, weights = section_backward(lax.dynamic_index_in_dim(layer_inputs, section, 0, False), incoming[direction], lax.dynamic_index_in_dim(gate_weight, section, 0, False), lax.dynamic_index_in_dim(up_weight, section, 0, False), lax.dynamic_index_in_dim(down_weight, section, 0, False))
            backs.append(back)
            totals.append(weights)
        lower_sum = [totals[0][which] + rounded(totals[1][which]) for which in range(3)]
        upper_sum = [totals[1][which] + rounded(totals[0][which]) for which in range(3)]
        lower = (momentum_decay * gate_momentum[sections[0]] + lower_sum[0][:HALF], momentum_decay * up_momentum[sections[0]] + lower_sum[1][:HALF], momentum_decay * down_momentum[sections[0]] + lower_sum[2][:, :HALF])
        upper = (momentum_decay * gate_momentum[sections[1]] + upper_sum[0][HALF:], momentum_decay * up_momentum[sections[1]] + upper_sum[1][HALF:], momentum_decay * down_momentum[sections[1]] + upper_sum[2][:, HALF:])
        stacked = jnp.stack(backs)
        return (stacked, (stacked, lower, upper))
    positions = jnp.arange(LAYERS, dtype=jnp.int32)
    _, (backs, lower, upper) = lax.scan(step, cotangent, positions)
    input_gradient = backs.reshape((2 * LAYERS,) + backs.shape[2:])
    results = []
    for which in range(3):
        paired = jnp.stack([lower[which], upper[which]], axis=1)
        results.append(paired.reshape((2 * LAYERS,) + paired.shape[2:]))
    return (input_gradient, results[0], results[1], results[2])
```

```python
import functools
import jax
import jax.numpy as jnp
from jax import lax
from jax.experimental import pallas as pl
from jax.experimental.pallas import tpu as pltpu
from jax.sharding import PartitionSpec as P

epsilon = 1e-05
momentum_decay = 0.9


def passed_along(block, axis, distance):
    devices = range(lax.axis_size(axis))
    route = [(i - distance, i) for i in devices if i - distance in devices]
    return lax.ppermute(block, axis, route)


def partner(block, axis, distance):
    count = lax.axis_size(axis)
    route = []
    for low in range(count):
        high = low | 1 << distance
        if high != low and high < count:
            route += [(low, high), (high, low)]
    return lax.ppermute(block, axis, route)


def contract_last(left, right):
    return lax.dot_general(
        left, right, (((1,), (1,)), ((), ())), preferred_element_type=jnp.float32
    )


def contract_rows(left, right):
    return lax.dot_general(
        left, right, (((0,), (0,)), ((), ())), preferred_element_type=jnp.float32
    )


def rounded(values):
    return lax.optimization_barrier(values.astype(jnp.bfloat16)).astype(jnp.float32)


def project(rows, gate_w, up_w):
    gate = jnp.dot(rows, gate_w, preferred_element_type=jnp.float32)
    up = jnp.dot(rows, up_w, preferred_element_type=jnp.float32)
    return (gate, up)


def backward_factors(incoming_rows, gate, up, down_w):
    hidden_grad = contract_last(incoming_rows, down_w)
    sigma = jax.nn.sigmoid(gate)
    silu = gate * sigma
    hidden = (silu * up).astype(jnp.bfloat16)
    gate_grad = (hidden_grad * up * sigma * (1.0 + gate * (1.0 - sigma))).astype(jnp.bfloat16)
    up_grad = (hidden_grad * silu).astype(jnp.bfloat16)
    return (hidden, gate_grad, up_grad)


def owned(array, start, size, axis):
    return lax.dynamic_slice_in_dim(array, start, size, axis)


def shards(
    layer_inputs,
    cotangent,
    gate_weight,
    up_weight,
    down_weight,
    gate_momentum,
    up_momentum,
    down_momentum,
):
    segments = lax.axis_size("segment")
    depth = segments // 2
    segment = lax.axis_index("segment")
    direction = segment % 2
    lower = direction == 0
    position = segment // 2
    gate_w = gate_weight[0]
    up_w = up_weight[0]
    down_w = down_weight[0]
    inputs = layer_inputs[0].astype(jnp.float32)
    micro, rows_dev, width = inputs.shape
    half = width // 2
    hidden_dev = gate_w.shape[1]
    total_rows = rows_dev * lax.axis_size("tp")
    inverse_norm = lax.rsqrt(jnp.mean(inputs * inputs, axis=-1, keepdims=True) + epsilon)
    exact = inputs * inverse_norm
    normed = exact.astype(jnp.bfloat16)
    entry = lax.dynamic_index_in_dim(cotangent, direction, 0, keepdims=False)
    ticks = depth + micro - 1
    wide_store = jnp.zeros((micro, total_rows, width), jnp.bfloat16)
    narrow_store = jnp.zeros((micro, total_rows, hidden_dev), jnp.bfloat16)
    extra = (wide_store, narrow_store, narrow_store, narrow_store) + (wide_store,)

    def process(tick, received, state):
        outgoing, backs, extra = state
        index = tick - position
        active = (index >= 0) & (index < micro)
        slot = jnp.clip(index, 0, micro - 1)
        local_in = jnp.where(position == 0, entry[slot], received)
        incoming_rows = lax.all_gather(local_in, "tp", axis=0, tiled=True)
        full_rows = lax.all_gather(normed[slot], "tp", axis=0, tiled=True)

        def factors():
            gate, up = project(full_rows, gate_w, up_w)
            return backward_factors(incoming_rows, gate, up, down_w)

        def resting():
            blank = jnp.zeros((total_rows, hidden_dev), jnp.bfloat16)
            return (blank, blank, blank)

        hidden, gate_grad, up_grad = lax.cond(active, factors, resting)
        count = lax.axis_size("tp") * rows_dev

        def compute():
            return contract_last(gate_grad, gate_w) + contract_last(up_grad, up_w)

        def quiet():
            return jnp.zeros((count, width), jnp.float32)

        normed_grad = lax.psum_scatter(
            lax.cond(active, compute, quiet).astype(jnp.bfloat16),
            "tp",
            scatter_dimension=0,
            tiled=True,
        ).astype(jnp.float32)
        scale = inverse_norm[slot]
        base = exact[slot]
        back = local_in.astype(jnp.float32) + scale * (
            normed_grad - base * jnp.mean(normed_grad * base, axis=-1, keepdims=True)
        )
        back = back.astype(jnp.bfloat16)
        backs = lax.dynamic_update_index_in_dim(
            backs, jnp.where(active, back, backs[slot]), slot, 0
        )
        fresh = (incoming_rows, hidden, gate_grad, up_grad) + (full_rows,)
        extra = tuple(
            (
                lax.dynamic_update_index_in_dim(
                    store, jnp.where(active, item, store[slot]), slot, 0
                )
                for store, item in zip(extra, fresh)
            )
        )
        return (back, backs, extra)

    zero_rows = jnp.zeros((rows_dev, width), jnp.bfloat16)
    state = process(
        0, zero_rows, (zero_rows, jnp.zeros((micro, rows_dev, width), jnp.bfloat16), extra)
    )

    def advance(tick, state):
        received = passed_along(state[0], "segment", 2)
        return process(tick, received, state)

    outgoing, backs, extra = lax.fori_loop(1, ticks, advance, state)
    keep_start = jnp.where(lower, 0, half)
    send_start = half - keep_start
    flat_rows = micro * total_rows
    normed_all = extra[4]
    normed_flat = normed_all.reshape(flat_rows, width)
    incoming_flat = extra[0].reshape(flat_rows, width)
    hidden_flat = extra[1].reshape(flat_rows, hidden_dev)
    gate_flat = extra[2].reshape(flat_rows, hidden_dev)
    up_flat = extra[3].reshape(flat_rows, hidden_dev)
    arrived = partner(
        (
            owned(normed_flat, send_start, half, 1),
            owned(incoming_flat, send_start, half, 1),
            hidden_flat,
            gate_flat,
            up_flat,
        ),
        "segment",
        0,
    )
    normed_keep = owned(normed_flat, keep_start, half, 1)
    incoming_keep = owned(incoming_flat, keep_start, half, 1)
    gate_share = contract_rows(normed_keep, gate_flat) + rounded(
        contract_rows(arrived[0], arrived[3])
    )
    up_share = contract_rows(normed_keep, up_flat) + rounded(contract_rows(arrived[0], arrived[4]))
    down_share = contract_rows(hidden_flat, incoming_keep) + rounded(
        contract_rows(arrived[2], arrived[1])
    )
    new_gate = (momentum_decay * gate_momentum[0] + gate_share)[None]
    new_up = (momentum_decay * up_momentum[0] + up_share)[None]
    new_down = (momentum_decay * down_momentum[0] + down_share)[None]
    return (backs[None], new_gate, new_up, new_down)


def masks_even(count):
    return sorted(range(2, count, 2), key=lambda m: -(m & -m))


def relay_kernel(
    n,
    depth,
    li_ref,
    cot_ref,
    gate_hbm,
    up_hbm,
    down_hbm,
    back_ref,
    normed_out,
    incoming_out,
    hidden_out,
    gate_out,
    up_out,
    gate_w,
    up_w,
    down_w,
    nrm,
    inc,
    slope,
    silu_s,
    exact_s,
    inv_s,
    parts,
    rs_recv,
    z_send,
    load_sem,
    ssem,
    rsem,
):
    micro, rows, width = li_ref.shape
    hid = down_w.shape[0]
    total = n * rows
    half = width // 2
    bits = n.bit_length() - 1
    s = lax.axis_index("segment")
    t = lax.axis_index("tp")
    p = lax.div(s, 2)
    d = lax.rem(s, 2)
    mirror = s + 1 - 2 * d

    def flip(mask):
        value = t
        for b in range(bits):
            if mask >> b & 1:
                value = value + (1 << b) * (1 - 2 * lax.rem(lax.div(t, 1 << b), 2))
        return value

    def copy(k, kind, slot, src, dst, device):
        return pltpu.make_async_remote_copy(
            src_ref=src,
            dst_ref=dst,
            send_sem=ssem.at[k, kind * n + slot],
            recv_sem=rsem.at[k, kind * n + slot],
            device_id=device,
            device_id_type=pl.DeviceIdType.MESH,
        )

    loads = [
        pltpu.make_async_copy(a, b, load_sem.at[i])
        for i, (a, b) in enumerate(((gate_hbm, gate_w), (up_hbm, up_w), (down_hbm, down_w)))
    ]
    for load in loads:
        load.start()

    barrier = pltpu.get_barrier_semaphore()

    def greet(device):
        pl.semaphore_signal(
            barrier, inc=1, device_id=device, device_id_type=pl.DeviceIdType.MESH
        )

    for b in range(bits):
        greet({"tp": flip(1 << b)})
    greet({"segment": mirror})

    @pl.when(p > 0)
    def _():
        greet({"segment": s - 2})

    @pl.when(p < depth - 1)
    def _():
        greet({"segment": s + 2})

    for k in range(micro):
        x = li_ref[k].astype(jnp.float32)
        inv = lax.rsqrt(jnp.mean(x * x, axis=-1, keepdims=True) + epsilon)
        exact = x * inv
        inv_s[k] = inv
        exact_s[k] = exact
        nrm[0, k, t] = exact.astype(jnp.bfloat16)

    peers = bits + 1 + jnp.minimum(p, 1) + jnp.minimum(depth - 1 - p, 1)
    pl.semaphore_wait(barrier, peers)

    def ag_copy(kind, k, m, b):
        buf = (nrm, inc)[kind]
        block = buf.at[0, k, flip(m)]
        return copy(k, kind, m | 1 << b, block, block, {"tp": flip(1 << b)})

    def ag_arrival(kind, k, slot):
        buf = (nrm, inc)[kind]
        block = buf.at[0, k, flip(slot)]
        low = slot & -slot
        return copy(k, kind, slot, block, block, {"tp": flip(low)})

    def ag_start(kind, k):
        for b in reversed(range(bits)):
            ag_copy(kind, k, 0, b).start()

    def ag_forward(kind, k):
        for m in masks_even(n):
            ag_arrival(kind, k, m).wait_recv()
            for b in reversed(range(bits)):
                if 1 << b < (m & -m):
                    ag_copy(kind, k, m, b).start()

    def ag_finish(kind, k):
        for m in range(1, n, 2):
            ag_arrival(kind, k, m).wait_recv()

    def mirror_copy(kind, k):
        buf = (nrm, inc)[kind]
        return copy(k, kind, 0, buf.at[0, k], buf.at[1, k], {"segment": mirror})

    def forward(side, k):
        start = (side * micro + k) * total
        lhs = nrm[side, k].reshape(total, width)
        step = min(256, hid)

        @pl.loop(0, hid // step)
        def _(j):
            cols = pl.ds(pl.multiple_of(j * step, step), step)
            g = jnp.dot(lhs, gate_w[:, cols], preferred_element_type=jnp.float32)
            u = jnp.dot(lhs, up_w[:, cols], preferred_element_type=jnp.float32)
            sigma = jax.nn.sigmoid(g)
            sl = g * sigma
            hidden_out[start : start + total, cols] = (sl * u).astype(jnp.bfloat16)
            slope[start : start + total, cols] = u * sigma * (1.0 + g * (1.0 - sigma))
            silu_s[start : start + total, cols] = sl

        keep = pl.ds(pl.multiple_of(d * half, half), half)
        normed_out[start : start + total, :] = nrm[side, k, :, :, keep].reshape(total, half)

    def factors(side, k):
        start = (side * micro + k) * total
        lhs = inc[side, k].reshape(total, width)
        step = min(256, hid)

        @pl.loop(0, hid // step)
        def _(j):
            cols = pl.ds(pl.multiple_of(j * step, step), step)
            grad = contract_last(lhs, down_w[cols, :])
            gate_out[start : start + total, cols] = (
                grad * slope[start : start + total, cols]
            ).astype(jnp.bfloat16)
            up_out[start : start + total, cols] = (
                grad * silu_s[start : start + total, cols]
            ).astype(jnp.bfloat16)

    def keep_incoming(side, k):
        start = (side * micro + k) * total
        keep = pl.ds(pl.multiple_of(d * half, half), half)
        incoming_out[start : start + total, :] = inc[side, k, :, :, keep].reshape(total, half)

    def partial_grads(k):
        start = k * total
        gg = gate_out[start : start + total, :]
        ug = up_out[start : start + total, :]
        step = min(256, width)

        @pl.loop(0, width // step)
        def _(j):
            cols = pl.ds(pl.multiple_of(j * step, step), step)
            part = contract_last(gg, gate_w[cols, :]) + contract_last(ug, up_w[cols, :])
            parts[k, :, :, cols] = part.astype(jnp.bfloat16).reshape(n, rows, step)

    def rs_copy(k, b, m):
        q = m | 1 << b
        return copy(k, 2, q, parts.at[k, flip(q)], rs_recv.at[k, q], {"tp": flip(1 << b)})

    def rs_round(k, b):
        for m in range(0, n, 1 << (b + 1)):
            q = m | 1 << b
            if b:
                value = parts[k, flip(q)].astype(jnp.float32)
                for lower in range(b):
                    value = value + rs_recv[k, q | 1 << lower].astype(jnp.float32)
                parts[k, flip(q)] = value.astype(jnp.bfloat16)
            rs_copy(k, b, m).start()

    def rs_wait(k, b):
        for m in range(0, n, 1 << (b + 1)):
            rs_copy(k, b, m).wait_recv()

    def z_copy(k):
        return copy(k, 2, 0, z_send.at[k], inc.at[0, k, t], {"segment": s + 2})

    def z_arrival(k):
        return copy(k, 2, 0, z_send.at[k], inc.at[0, k, t], {"segment": s - 2})

    def finish(k):
        value = parts[k, t].astype(jnp.float32)
        for b in range(bits):
            value = value + rs_recv[k, 1 << b].astype(jnp.float32)
        base = exact_s[k]
        back = inc[0, k, t].astype(jnp.float32) + inv_s[k] * (
            value - base * jnp.mean(value * base, axis=-1, keepdims=True)
        )
        back = back.astype(jnp.bfloat16)
        z_send[k] = back

        @pl.when(p < depth - 1)
        def _():
            z_copy(k).start()

        back_ref[k] = back

    first = p == 0
    early = p * 2 >= depth

    for k in range(micro):
        ag_start(0, k)

        @pl.when(first)
        def _():
            inc[0, k, t] = cot_ref[d, k]
            ag_start(1, k)

    def mirror_forward():
        for k in range(micro):
            mirror_copy(0, k).wait_recv()
            forward(1, k)

    for k in range(micro):
        ag_forward(0, k)

        @pl.when(first)
        def _():
            ag_forward(1, k)

        ag_finish(0, k)
        mirror_copy(0, k).start()
        if k == 0:
            loads[0].wait()
            loads[1].wait()
            forward(0, k)
        if k == 0:
            loads[2].wait()

    @pl.when(jnp.logical_not(first))
    def _():
        for k in range(1, micro):
            forward(0, k)

    @pl.when(early)
    def _():
        mirror_forward()

    def receive(k):
        @pl.when(jnp.logical_not(first))
        def _():
            z_arrival(k).wait_recv()
            ag_start(1, k)

    def relay(k):
        @pl.when(jnp.logical_not(first))
        def _():
            ag_forward(1, k)

    def compute(k):
        ag_finish(1, k)
        mirror_copy(1, k).start()
        factors(0, k)
        partial_grads(k)
        rs_round(k, 0)
        keep_incoming(0, k)

    def reduce(k):
        for b in range(1, bits):
            rs_wait(k, b - 1)
            rs_round(k, b)

    def end(k):
        rs_wait(k, bits - 1)
        finish(k)

    def mirror_factors(k):
        mirror_copy(1, k).wait_recv()
        factors(1, k)
        keep_incoming(1, k)

    receive(0)
    relay(0)
    compute(0)

    @pl.when(first)
    def _():
        for k in range(1, micro):
            forward(0, k)

    for k in range(1, micro):
        receive(k)
        reduce(k - 1)
        relay(k)
        end(k - 1)
        compute(k)
    reduce(micro - 1)

    @pl.when(early)
    def _():
        for k in range(micro - 1):
            mirror_factors(k)

    end(micro - 1)

    @pl.when(jnp.logical_not(early))
    def _():
        mirror_forward()
        for k in range(micro - 1):
            mirror_factors(k)

    mirror_factors(micro - 1)

    for k in range(micro):
        for kind in range(2):
            mirror_copy(kind, k).wait_send()
            for b in range(bits):
                for m in range(0, n, 1 << (b + 1)):
                    ag_copy(kind, k, m, b).wait_send()
        for b in range(bits):
            for m in range(0, n, 1 << (b + 1)):
                rs_copy(k, b, m).wait_send()

        @pl.when(p < depth - 1)
        def _():
            z_copy(k).wait_send()


def relayed(
    segments,
    n,
    layer_inputs,
    cotangent,
    gate_weight,
    up_weight,
    down_weight,
    gate_momentum,
    up_momentum,
    down_momentum,
):
    _, micro, rows, width = layer_inputs.shape
    hid = gate_weight.shape[2]
    half = width // 2
    flat = 2 * micro * n * rows
    vmem = pl.BlockSpec(memory_space=pltpu.VMEM)
    hbm = pl.BlockSpec(memory_space=pl.ANY)
    bf, f32 = jnp.bfloat16, jnp.float32
    back, normed, incoming, hidden, gate, up = pl.pallas_call(
        functools.partial(relay_kernel, n, segments // 2),
        name="relay",
        out_shape=(
            jax.ShapeDtypeStruct((micro, rows, width), bf),
            jax.ShapeDtypeStruct((flat, half), bf),
            jax.ShapeDtypeStruct((flat, half), bf),
            jax.ShapeDtypeStruct((flat, hid), bf),
            jax.ShapeDtypeStruct((flat, hid), bf),
            jax.ShapeDtypeStruct((flat, hid), bf),
        ),
        in_specs=[vmem, vmem, hbm, hbm, hbm],
        out_specs=(vmem,) * 6,
        scratch_shapes=[
            pltpu.VMEM((width, hid), bf),
            pltpu.VMEM((width, hid), bf),
            pltpu.VMEM((hid, width), bf),
            pltpu.VMEM((2, micro, n, rows, width), bf),
            pltpu.VMEM((2, micro, n, rows, width), bf),
            pltpu.VMEM((flat, hid), f32),
            pltpu.VMEM((flat, hid), f32),
            pltpu.VMEM((micro, rows, width), f32),
            pltpu.VMEM((micro, rows, 1), f32),
            pltpu.VMEM((micro, n, rows, width), bf),
            pltpu.VMEM((micro, n, rows, width), bf),
            pltpu.VMEM((micro, rows, width), bf),
            pltpu.SemaphoreType.DMA((3,)),
            pltpu.SemaphoreType.DMA((micro, 3 * n)),
            pltpu.SemaphoreType.DMA((micro, 3 * n)),
        ],
        compiler_params=pltpu.CompilerParams(
            collective_id=0, has_side_effects=True, vmem_limit_bytes=56 << 20
        ),
    )(layer_inputs[0], cotangent, gate_weight[0], up_weight[0], down_weight[0])
    new_gate = momentum_decay * gate_momentum[0] + contract_rows(normed, gate)
    new_up = momentum_decay * up_momentum[0] + contract_rows(normed, up)
    new_down = momentum_decay * down_momentum[0] + contract_rows(hidden, incoming)
    return (back[None], new_gate[None], new_up[None], new_down[None])


def choose(segments, n, *arrays):
    rows = arrays[0].shape[2]
    if rows % 16 == 0 and n > 1 and n & (n - 1) == 0:
        return relayed(segments, n, *arrays)
    return shards(*arrays)


def solution(mesh):
    body = functools.partial(choose, mesh.shape["segment"], mesh.shape["tp"])
    return jax.shard_map(
        body,
        mesh=mesh,
        in_specs=(
            P("segment", None, "tp", None),
            P(None, None, "tp", None),
            P("segment", None, "tp"),
            P("segment", None, "tp"),
            P("segment", "tp", None),
            P("segment", None, "tp"),
            P("segment", None, "tp"),
            P("segment", "tp", None),
        ),
        out_specs=(
            P("segment", None, "tp", None),
            P("segment", None, "tp"),
            P("segment", None, "tp"),
            P("segment", "tp", None),
        ),
        check_vma=False,
    )
```

```python
import functools
import jax
import jax.numpy as jnp
from jax import lax
from jax.experimental import pallas as pl
from jax.experimental.pallas import tpu as pltpu
from jax.sharding import PartitionSpec as P

epsilon = 1e-05
momentum_decay = 0.9


def passed_along(block, axis, distance):
    devices = range(lax.axis_size(axis))
    route = [(i - distance, i) for i in devices if i - distance in devices]
    return lax.ppermute(block, axis, route)


def partner(block, axis, distance):
    count = lax.axis_size(axis)
    route = []
    for low in range(count):
        high = low | 1 << distance
        if high != low and high < count:
            route += [(low, high), (high, low)]
    return lax.ppermute(block, axis, route)


def contract_last(left, right):
    return lax.dot_general(
        left, right, (((1,), (1,)), ((), ())), preferred_element_type=jnp.float32
    )


def contract_rows(left, right):
    return lax.dot_general(
        left, right, (((0,), (0,)), ((), ())), preferred_element_type=jnp.float32
    )


def rounded(values):
    return lax.optimization_barrier(values.astype(jnp.bfloat16)).astype(jnp.float32)


def project(rows, gate_w, up_w):
    gate = jnp.dot(rows, gate_w, preferred_element_type=jnp.float32)
    up = jnp.dot(rows, up_w, preferred_element_type=jnp.float32)
    return (gate, up)


def backward_factors(incoming_rows, gate, up, down_w):
    hidden_grad = contract_last(incoming_rows, down_w)
    sigma = jax.nn.sigmoid(gate)
    silu = gate * sigma
    hidden = (silu * up).astype(jnp.bfloat16)
    gate_grad = (hidden_grad * up * sigma * (1.0 + gate * (1.0 - sigma))).astype(jnp.bfloat16)
    up_grad = (hidden_grad * silu).astype(jnp.bfloat16)
    return (hidden, gate_grad, up_grad)


def owned(array, start, size, axis):
    return lax.dynamic_slice_in_dim(array, start, size, axis)


def shards(
    layer_inputs,
    cotangent,
    gate_weight,
    up_weight,
    down_weight,
    gate_momentum,
    up_momentum,
    down_momentum,
):
    segments = lax.axis_size("segment")
    depth = segments // 2
    segment = lax.axis_index("segment")
    direction = segment % 2
    lower = direction == 0
    position = segment // 2
    gate_w = gate_weight[0]
    up_w = up_weight[0]
    down_w = down_weight[0]
    inputs = layer_inputs[0].astype(jnp.float32)
    micro, rows_dev, width = inputs.shape
    half = width // 2
    hidden_dev = gate_w.shape[1]
    total_rows = rows_dev * lax.axis_size("tp")
    inverse_norm = lax.rsqrt(jnp.mean(inputs * inputs, axis=-1, keepdims=True) + epsilon)
    exact = inputs * inverse_norm
    normed = exact.astype(jnp.bfloat16)
    entry = lax.dynamic_index_in_dim(cotangent, direction, 0, keepdims=False)
    ticks = depth + micro - 1
    wide_store = jnp.zeros((micro, total_rows, width), jnp.bfloat16)
    narrow_store = jnp.zeros((micro, total_rows, hidden_dev), jnp.bfloat16)
    extra = (wide_store, narrow_store, narrow_store, narrow_store) + (wide_store,)

    def process(tick, received, state):
        outgoing, backs, extra = state
        index = tick - position
        active = (index >= 0) & (index < micro)
        slot = jnp.clip(index, 0, micro - 1)
        local_in = jnp.where(position == 0, entry[slot], received)
        incoming_rows = lax.all_gather(local_in, "tp", axis=0, tiled=True)
        full_rows = lax.all_gather(normed[slot], "tp", axis=0, tiled=True)

        def factors():
            gate, up = project(full_rows, gate_w, up_w)
            return backward_factors(incoming_rows, gate, up, down_w)

        def resting():
            blank = jnp.zeros((total_rows, hidden_dev), jnp.bfloat16)
            return (blank, blank, blank)

        hidden, gate_grad, up_grad = lax.cond(active, factors, resting)
        count = lax.axis_size("tp") * rows_dev

        def compute():
            return contract_last(gate_grad, gate_w) + contract_last(up_grad, up_w)

        def quiet():
            return jnp.zeros((count, width), jnp.float32)

        normed_grad = lax.psum_scatter(
            lax.cond(active, compute, quiet).astype(jnp.bfloat16),
            "tp",
            scatter_dimension=0,
            tiled=True,
        ).astype(jnp.float32)
        scale = inverse_norm[slot]
        base = exact[slot]
        back = local_in.astype(jnp.float32) + scale * (
            normed_grad - base * jnp.mean(normed_grad * base, axis=-1, keepdims=True)
        )
        back = back.astype(jnp.bfloat16)
        backs = lax.dynamic_update_index_in_dim(
            backs, jnp.where(active, back, backs[slot]), slot, 0
        )
        fresh = (incoming_rows, hidden, gate_grad, up_grad) + (full_rows,)
        extra = tuple(
            (
                lax.dynamic_update_index_in_dim(
                    store, jnp.where(active, item, store[slot]), slot, 0
                )
                for store, item in zip(extra, fresh)
            )
        )
        return (back, backs, extra)

    zero_rows = jnp.zeros((rows_dev, width), jnp.bfloat16)
    state = process(
        0, zero_rows, (zero_rows, jnp.zeros((micro, rows_dev, width), jnp.bfloat16), extra)
    )

    def advance(tick, state):
        received = passed_along(state[0], "segment", 2)
        return process(tick, received, state)

    outgoing, backs, extra = lax.fori_loop(1, ticks, advance, state)
    keep_start = jnp.where(lower, 0, half)
    send_start = half - keep_start
    flat_rows = micro * total_rows
    normed_all = extra[4]
    normed_flat = normed_all.reshape(flat_rows, width)
    incoming_flat = extra[0].reshape(flat_rows, width)
    hidden_flat = extra[1].reshape(flat_rows, hidden_dev)
    gate_flat = extra[2].reshape(flat_rows, hidden_dev)
    up_flat = extra[3].reshape(flat_rows, hidden_dev)
    arrived = partner(
        (
            owned(normed_flat, send_start, half, 1),
            owned(incoming_flat, send_start, half, 1),
            hidden_flat,
            gate_flat,
            up_flat,
        ),
        "segment",
        0,
    )
    normed_keep = owned(normed_flat, keep_start, half, 1)
    incoming_keep = owned(incoming_flat, keep_start, half, 1)
    gate_share = contract_rows(normed_keep, gate_flat) + rounded(
        contract_rows(arrived[0], arrived[3])
    )
    up_share = contract_rows(normed_keep, up_flat) + rounded(contract_rows(arrived[0], arrived[4]))
    down_share = contract_rows(hidden_flat, incoming_keep) + rounded(
        contract_rows(arrived[2], arrived[1])
    )
    new_gate = (momentum_decay * gate_momentum[0] + gate_share)[None]
    new_up = (momentum_decay * up_momentum[0] + up_share)[None]
    new_down = (momentum_decay * down_momentum[0] + down_share)[None]
    return (backs[None], new_gate, new_up, new_down)


def masks_even(count):
    return sorted(range(2, count, 2), key=lambda m: -(m & -m))


def relay_kernel(
    n,
    depth,
    li_ref,
    cot_ref,
    gate_hbm,
    up_hbm,
    down_hbm,
    back_ref,
    normed_out,
    incoming_out,
    hidden_out,
    gate_out,
    up_out,
    gate_w,
    up_w,
    down_w,
    nrm,
    inc,
    slope,
    silu_s,
    exact_s,
    inv_s,
    parts,
    rs_recv,
    z_send,
    gate_t,
    up_t,
    down_t,
    load_sem,
    ssem,
    rsem,
):
    micro, rows, width = li_ref.shape
    hid = down_w.shape[0]
    total = n * rows
    half = width // 2
    bits = n.bit_length() - 1
    pieces = ssem.shape[1]
    size = rows // pieces
    s = lax.axis_index("segment")
    t = lax.axis_index("tp")
    p = lax.div(s, 2)
    d = lax.rem(s, 2)
    mirror = s + 1 - 2 * d

    def flip(mask):
        value = t
        for b in range(bits):
            if mask >> b & 1:
                value = value + (1 << b) * (1 - 2 * lax.rem(lax.div(t, 1 << b), 2))
        return value

    def piece(c):
        return pl.ds(c * size, size)

    def copy(k, c, kind, slot, src, dst, device):
        return pltpu.make_async_remote_copy(
            src_ref=src,
            dst_ref=dst,
            send_sem=ssem.at[k, c, kind * n + slot],
            recv_sem=rsem.at[k, c, kind * n + slot],
            device_id=device,
            device_id_type=pl.DeviceIdType.MESH,
        )

    loads = [
        pltpu.make_async_copy(a, b, load_sem.at[i])
        for i, (a, b) in enumerate(((gate_hbm, gate_w), (up_hbm, up_w), (down_hbm, down_w)))
    ]
    for load in loads:
        load.start()

    barrier = pltpu.get_barrier_semaphore()

    def greet(device):
        pl.semaphore_signal(
            barrier, inc=1, device_id=device, device_id_type=pl.DeviceIdType.MESH
        )

    for b in range(bits):
        greet({"tp": flip(1 << b)})
    greet({"segment": mirror})

    @pl.when(p > 0)
    def _():
        greet({"segment": s - 2})

    @pl.when(p < depth - 1)
    def _():
        greet({"segment": s + 2})

    for k in range(micro):
        x = li_ref[k].astype(jnp.float32)
        inv = lax.rsqrt(jnp.mean(x * x, axis=-1, keepdims=True) + epsilon)
        exact = x * inv
        inv_s[k] = inv
        exact_s[k] = exact
        nrm[0, k, t] = exact.astype(jnp.bfloat16)

    peers = bits + 1 + jnp.minimum(p, 1) + jnp.minimum(depth - 1 - p, 1)
    pl.semaphore_wait(barrier, peers)

    def ag_copy(kind, k, c, m, b):
        buf = (nrm, inc)[kind]
        block = buf.at[0, k, flip(m), piece(c)]
        return copy(k, c, kind, m | 1 << b, block, block, {"tp": flip(1 << b)})

    def ag_arrival(kind, k, c, slot):
        buf = (nrm, inc)[kind]
        block = buf.at[0, k, flip(slot), piece(c)]
        low = slot & -slot
        return copy(k, c, kind, slot, block, block, {"tp": flip(low)})

    def ag_start(kind, k, c):
        for b in reversed(range(bits)):
            ag_copy(kind, k, c, 0, b).start()

    def ag_forward(kind, k):
        for c in range(pieces):
            for m in masks_even(n):
                ag_arrival(kind, k, c, m).wait_recv()
                for b in reversed(range(bits)):
                    if 1 << b < (m & -m):
                        ag_copy(kind, k, c, m, b).start()

    def ag_finish(kind, k):
        for c in range(pieces):
            for m in range(1, n, 2):
                ag_arrival(kind, k, c, m).wait_recv()

    def mirror_copy(kind, k):
        buf = (nrm, inc)[kind]
        return copy(k, 0, kind, 0, buf.at[0, k], buf.at[1, k], {"segment": mirror})

    def forward(side, k):
        start = (side * micro + k) * total
        lhs = nrm[side, k].reshape(total, width)
        step = min(256, hid)

        @pl.loop(0, hid // step)
        def _(j):
            cols = pl.ds(pl.multiple_of(j * step, step), step)
            g = jnp.dot(lhs, gate_w[:, cols], preferred_element_type=jnp.float32)
            u = jnp.dot(lhs, up_w[:, cols], preferred_element_type=jnp.float32)
            sigma = jax.nn.sigmoid(g)
            sl = g * sigma
            hidden_out[start : start + total, cols] = (sl * u).astype(jnp.bfloat16)
            slope[start : start + total, cols] = u * sigma * (1.0 + g * (1.0 - sigma))
            silu_s[start : start + total, cols] = sl

        keep = pl.ds(pl.multiple_of(d * half, half), half)
        normed_out[start : start + total, :] = nrm[side, k, :, :, keep].reshape(total, half)

    def factors(side, k, turned):
        start = (side * micro + k) * total
        lhs = inc[side, k].reshape(total, width)
        step = min(512, hid)

        @pl.loop(0, hid // step)
        def _(j):
            cols = pl.ds(pl.multiple_of(j * step, step), step)
            if turned:
                grad = jnp.dot(lhs, down_t[:, cols], preferred_element_type=jnp.float32)
            else:
                grad = contract_last(lhs, down_w[cols, :])
            gate_out[start : start + total, cols] = (
                grad * slope[start : start + total, cols]
            ).astype(jnp.bfloat16)
            up_out[start : start + total, cols] = (
                grad * silu_s[start : start + total, cols]
            ).astype(jnp.bfloat16)

    def keep_incoming(side, k):
        start = (side * micro + k) * total
        keep = pl.ds(pl.multiple_of(d * half, half), half)
        incoming_out[start : start + total, :] = inc[side, k, :, :, keep].reshape(total, half)

    def partial_grads(k, turned):
        start = k * total
        step = min(512, width)

        @pl.loop(0, width // step)
        def _(j):
            gg = gate_out[start : start + total, :]
            ug = up_out[start : start + total, :]
            cols = pl.ds(pl.multiple_of(j * step, step), step)
            if turned:
                part = jnp.dot(gg, gate_t[:, cols], preferred_element_type=jnp.float32)
                part = part + jnp.dot(ug, up_t[:, cols], preferred_element_type=jnp.float32)
            else:
                part = contract_last(gg, gate_w[cols, :]) + contract_last(ug, up_w[cols, :])
            parts[k, :, :, cols] = part.astype(jnp.bfloat16).reshape(n, rows, step)

    def turn(source, target):
        step = 256

        @pl.loop(0, source.shape[1] // step)
        def _(j):
            cols = pl.ds(pl.multiple_of(j * step, step), step)
            target[cols, :] = source[:, cols].T

    def rs_copy(k, c, b, m):
        q = m | 1 << b
        src = parts.at[k, flip(q), piece(c)]
        return copy(k, c, 2, q, src, rs_recv.at[k, q, piece(c)], {"tp": flip(1 << b)})

    def rs_round(k, c, b):
        for m in range(0, n, 1 << (b + 1)):
            q = m | 1 << b
            if b:
                value = parts[k, flip(q), piece(c)].astype(jnp.float32)
                for lower in range(b):
                    value = value + rs_recv[k, q | 1 << lower, piece(c)].astype(jnp.float32)
                parts[k, flip(q), piece(c)] = value.astype(jnp.bfloat16)
            rs_copy(k, c, b, m).start()

    def rs_wait(k, c, b):
        for m in range(0, n, 1 << (b + 1)):
            rs_copy(k, c, b, m).wait_recv()

    def z_copy(k, c, step=2):
        dst = inc.at[0, k, t, piece(c)]
        return copy(k, c, 2, 0, z_send.at[k, piece(c)], dst, {"segment": s + step})

    def finish(k, c):
        span = piece(c)
        value = parts[k, t, span].astype(jnp.float32)
        for b in range(bits):
            value = value + rs_recv[k, 1 << b, span].astype(jnp.float32)
        base = exact_s[k, span]
        back = inc[0, k, t, span].astype(jnp.float32) + inv_s[k, span] * (
            value - base * jnp.mean(value * base, axis=-1, keepdims=True)
        )
        back = back.astype(jnp.bfloat16)
        z_send[k, span] = back

        @pl.when(p < depth - 1)
        def _():
            z_copy(k, c).start()

        back_ref[k, span] = back

    first = p == 0
    early = p * 2 >= depth

    for k in range(micro):
        for c in range(pieces):
            ag_start(0, k, c)

        @pl.when(first)
        def _():
            inc[0, k, t] = cot_ref[d, k]
            for c in range(pieces):
                ag_start(1, k, c)

    def mirror_forward():
        for k in range(micro):
            mirror_copy(0, k).wait_recv()
            forward(1, k)

    for k in range(micro):
        ag_forward(0, k)

        @pl.when(first)
        def _():
            ag_forward(1, k)

        ag_finish(0, k)
        mirror_copy(0, k).start()
        if k == 0:
            loads[0].wait()
            loads[1].wait()
            forward(0, k)
        if k == 0:
            loads[2].wait()

    @pl.when(jnp.logical_not(first))
    def _():
        turn(down_w, down_t)
        turn(gate_w, gate_t)
        turn(up_w, up_t)
        for k in range(1, micro):
            forward(0, k)

    @pl.when(early)
    def _():
        mirror_forward()

    def receive(k):
        @pl.when(jnp.logical_not(first))
        def _():
            for c in range(pieces):
                z_copy(k, c, -2).wait_recv()
                ag_start(1, k, c)

    def relay(k):
        @pl.when(jnp.logical_not(first))
        def _():
            ag_forward(1, k)

    def compute(k):
        ag_finish(1, k)
        mirror_copy(1, k).start()

        @pl.when(first)
        def _():
            factors(0, k, False)
            partial_grads(k, False)

        @pl.when(jnp.logical_not(first))
        def _():
            factors(0, k, True)
            partial_grads(k, True)

        for c in range(pieces):
            rs_round(k, c, 0)
        keep_incoming(0, k)

    def reduce(k):
        for b in range(1, bits):
            for c in range(pieces):
                rs_wait(k, c, b - 1)
                rs_round(k, c, b)

    def end(k):
        for c in range(pieces):
            rs_wait(k, c, bits - 1)
            finish(k, c)

    def mirror_factors(k):
        mirror_copy(1, k).wait_recv()
        factors(1, k, False)
        keep_incoming(1, k)

    receive(0)
    relay(0)
    compute(0)

    @pl.when(first)
    def _():
        for k in range(1, micro):
            forward(0, k)

    for k in range(1, micro):
        reduce(k - 1)
        receive(k)
        relay(k)
        end(k - 1)
        compute(k)
    reduce(micro - 1)

    @pl.when(early)
    def _():
        for k in range(micro - 1):
            mirror_factors(k)

    end(micro - 1)

    @pl.when(jnp.logical_not(early))
    def _():
        mirror_forward()
        for k in range(micro - 1):
            mirror_factors(k)

    mirror_factors(micro - 1)

    for k in range(micro):
        for kind in range(2):
            mirror_copy(kind, k).wait_send()
        for c in range(pieces):
            for b in range(bits):
                for m in range(0, n, 1 << (b + 1)):
                    for kind in range(2):
                        ag_copy(kind, k, c, m, b).wait_send()
                    rs_copy(k, c, b, m).wait_send()

            @pl.when(p < depth - 1)
            def _():
                z_copy(k, c).wait_send()


def relayed(
    segments,
    n,
    layer_inputs,
    cotangent,
    gate_weight,
    up_weight,
    down_weight,
    gate_momentum,
    up_momentum,
    down_momentum,
):
    _, micro, rows, width = layer_inputs.shape
    hid = gate_weight.shape[2]
    half = width // 2
    flat = 2 * micro * n * rows
    vmem = pl.BlockSpec(memory_space=pltpu.VMEM)
    hbm = pl.BlockSpec(memory_space=pl.ANY)
    pieces = 2 if rows % 32 == 0 else 1
    bf, f32 = jnp.bfloat16, jnp.float32
    back, normed, incoming, hidden, gate, up = pl.pallas_call(
        functools.partial(relay_kernel, n, segments // 2),
        name="relay",
        out_shape=(
            jax.ShapeDtypeStruct((micro, rows, width), bf),
            jax.ShapeDtypeStruct((flat, half), bf),
            jax.ShapeDtypeStruct((flat, half), bf),
            jax.ShapeDtypeStruct((flat, hid), bf),
            jax.ShapeDtypeStruct((flat, hid), bf),
            jax.ShapeDtypeStruct((flat, hid), bf),
        ),
        in_specs=[vmem, vmem, hbm, hbm, hbm],
        out_specs=(vmem,) * 6,
        scratch_shapes=[
            pltpu.VMEM((width, hid), bf),
            pltpu.VMEM((width, hid), bf),
            pltpu.VMEM((hid, width), bf),
            pltpu.VMEM((2, micro, n, rows, width), bf),
            pltpu.VMEM((2, micro, n, rows, width), bf),
            pltpu.VMEM((flat, hid), f32),
            pltpu.VMEM((flat, hid), f32),
            pltpu.VMEM((micro, rows, width), f32),
            pltpu.VMEM((micro, rows, 1), f32),
            pltpu.VMEM((micro, n, rows, width), bf),
            pltpu.VMEM((micro, n, rows, width), bf),
            pltpu.VMEM((micro, rows, width), bf),
            pltpu.VMEM((hid, width), bf),
            pltpu.VMEM((hid, width), bf),
            pltpu.VMEM((width, hid), bf),
            pltpu.SemaphoreType.DMA((3,)),
            pltpu.SemaphoreType.DMA((micro, pieces, 3 * n)),
            pltpu.SemaphoreType.DMA((micro, pieces, 3 * n)),
        ],
        compiler_params=pltpu.CompilerParams(
            collective_id=0, has_side_effects=True, vmem_limit_bytes=60 << 20
        ),
    )(layer_inputs[0], cotangent, gate_weight[0], up_weight[0], down_weight[0])
    new_gate = momentum_decay * gate_momentum[0] + contract_rows(normed, gate)
    new_up = momentum_decay * up_momentum[0] + contract_rows(normed, up)
    new_down = momentum_decay * down_momentum[0] + contract_rows(hidden, incoming)
    return (back[None], new_gate[None], new_up[None], new_down[None])


def choose(segments, n, *arrays):
    rows = arrays[0].shape[2]
    if rows % 16 == 0 and n > 1 and n & (n - 1) == 0:
        return relayed(segments, n, *arrays)
    return shards(*arrays)


def solution(mesh):
    body = functools.partial(choose, mesh.shape["segment"], mesh.shape["tp"])
    return jax.shard_map(
        body,
        mesh=mesh,
        in_specs=(
            P("segment", None, "tp", None),
            P(None, None, "tp", None),
            P("segment", None, "tp"),
            P("segment", None, "tp"),
            P("segment", "tp", None),
            P("segment", None, "tp"),
            P("segment", None, "tp"),
            P("segment", "tp", None),
        ),
        out_specs=(
            P("segment", None, "tp", None),
            P("segment", None, "tp"),
            P("segment", None, "tp"),
            P("segment", "tp", None),
        ),
        check_vma=False,
    )
```

```python
import functools
import jax
import jax.numpy as jnp
from jax import lax
from jax.experimental import pallas as pl
from jax.experimental.pallas import tpu as pltpu
from jax.sharding import PartitionSpec as P

epsilon = 1e-05
momentum_decay = 0.9


def passed_along(block, axis, distance):
    devices = range(lax.axis_size(axis))
    route = [(i - distance, i) for i in devices if i - distance in devices]
    return lax.ppermute(block, axis, route)


def partner(block, axis, distance):
    count = lax.axis_size(axis)
    route = []
    for low in range(count):
        high = low | 1 << distance
        if high != low and high < count:
            route += [(low, high), (high, low)]
    return lax.ppermute(block, axis, route)


def contract_last(left, right):
    return lax.dot_general(
        left, right, (((1,), (1,)), ((), ())), preferred_element_type=jnp.float32
    )


def contract_rows(left, right):
    return lax.dot_general(
        left, right, (((0,), (0,)), ((), ())), preferred_element_type=jnp.float32
    )


def rounded(values):
    return lax.optimization_barrier(values.astype(jnp.bfloat16)).astype(jnp.float32)


def project(rows, gate_w, up_w):
    gate = jnp.dot(rows, gate_w, preferred_element_type=jnp.float32)
    up = jnp.dot(rows, up_w, preferred_element_type=jnp.float32)
    return (gate, up)


def backward_factors(incoming_rows, gate, up, down_w):
    hidden_grad = contract_last(incoming_rows, down_w)
    sigma = jax.nn.sigmoid(gate)
    silu = gate * sigma
    hidden = (silu * up).astype(jnp.bfloat16)
    gate_grad = (hidden_grad * up * sigma * (1.0 + gate * (1.0 - sigma))).astype(jnp.bfloat16)
    up_grad = (hidden_grad * silu).astype(jnp.bfloat16)
    return (hidden, gate_grad, up_grad)


def owned(array, start, size, axis):
    return lax.dynamic_slice_in_dim(array, start, size, axis)


def shards(
    layer_inputs,
    cotangent,
    gate_weight,
    up_weight,
    down_weight,
    gate_momentum,
    up_momentum,
    down_momentum,
):
    segments = lax.axis_size("segment")
    depth = segments // 2
    segment = lax.axis_index("segment")
    direction = segment % 2
    lower = direction == 0
    position = segment // 2
    gate_w = gate_weight[0]
    up_w = up_weight[0]
    down_w = down_weight[0]
    inputs = layer_inputs[0].astype(jnp.float32)
    micro, rows_dev, width = inputs.shape
    half = width // 2
    hidden_dev = gate_w.shape[1]
    total_rows = rows_dev * lax.axis_size("tp")
    inverse_norm = lax.rsqrt(jnp.mean(inputs * inputs, axis=-1, keepdims=True) + epsilon)
    exact = inputs * inverse_norm
    normed = exact.astype(jnp.bfloat16)
    entry = lax.dynamic_index_in_dim(cotangent, direction, 0, keepdims=False)
    ticks = depth + micro - 1
    wide_store = jnp.zeros((micro, total_rows, width), jnp.bfloat16)
    narrow_store = jnp.zeros((micro, total_rows, hidden_dev), jnp.bfloat16)
    extra = (wide_store, narrow_store, narrow_store, narrow_store) + (wide_store,)

    def process(tick, received, state):
        outgoing, backs, extra = state
        index = tick - position
        active = (index >= 0) & (index < micro)
        slot = jnp.clip(index, 0, micro - 1)
        local_in = jnp.where(position == 0, entry[slot], received)
        incoming_rows = lax.all_gather(local_in, "tp", axis=0, tiled=True)
        full_rows = lax.all_gather(normed[slot], "tp", axis=0, tiled=True)

        def factors():
            gate, up = project(full_rows, gate_w, up_w)
            return backward_factors(incoming_rows, gate, up, down_w)

        def resting():
            blank = jnp.zeros((total_rows, hidden_dev), jnp.bfloat16)
            return (blank, blank, blank)

        hidden, gate_grad, up_grad = lax.cond(active, factors, resting)
        count = lax.axis_size("tp") * rows_dev

        def compute():
            return contract_last(gate_grad, gate_w) + contract_last(up_grad, up_w)

        def quiet():
            return jnp.zeros((count, width), jnp.float32)

        normed_grad = lax.psum_scatter(
            lax.cond(active, compute, quiet).astype(jnp.bfloat16),
            "tp",
            scatter_dimension=0,
            tiled=True,
        ).astype(jnp.float32)
        scale = inverse_norm[slot]
        base = exact[slot]
        back = local_in.astype(jnp.float32) + scale * (
            normed_grad - base * jnp.mean(normed_grad * base, axis=-1, keepdims=True)
        )
        back = back.astype(jnp.bfloat16)
        backs = lax.dynamic_update_index_in_dim(
            backs, jnp.where(active, back, backs[slot]), slot, 0
        )
        fresh = (incoming_rows, hidden, gate_grad, up_grad) + (full_rows,)
        extra = tuple(
            (
                lax.dynamic_update_index_in_dim(
                    store, jnp.where(active, item, store[slot]), slot, 0
                )
                for store, item in zip(extra, fresh)
            )
        )
        return (back, backs, extra)

    zero_rows = jnp.zeros((rows_dev, width), jnp.bfloat16)
    state = process(
        0, zero_rows, (zero_rows, jnp.zeros((micro, rows_dev, width), jnp.bfloat16), extra)
    )

    def advance(tick, state):
        received = passed_along(state[0], "segment", 2)
        return process(tick, received, state)

    outgoing, backs, extra = lax.fori_loop(1, ticks, advance, state)
    keep_start = jnp.where(lower, 0, half)
    send_start = half - keep_start
    flat_rows = micro * total_rows
    normed_all = extra[4]
    normed_flat = normed_all.reshape(flat_rows, width)
    incoming_flat = extra[0].reshape(flat_rows, width)
    hidden_flat = extra[1].reshape(flat_rows, hidden_dev)
    gate_flat = extra[2].reshape(flat_rows, hidden_dev)
    up_flat = extra[3].reshape(flat_rows, hidden_dev)
    arrived = partner(
        (
            owned(normed_flat, send_start, half, 1),
            owned(incoming_flat, send_start, half, 1),
            hidden_flat,
            gate_flat,
            up_flat,
        ),
        "segment",
        0,
    )
    normed_keep = owned(normed_flat, keep_start, half, 1)
    incoming_keep = owned(incoming_flat, keep_start, half, 1)
    gate_share = contract_rows(normed_keep, gate_flat) + rounded(
        contract_rows(arrived[0], arrived[3])
    )
    up_share = contract_rows(normed_keep, up_flat) + rounded(contract_rows(arrived[0], arrived[4]))
    down_share = contract_rows(hidden_flat, incoming_keep) + rounded(
        contract_rows(arrived[2], arrived[1])
    )
    new_gate = (momentum_decay * gate_momentum[0] + gate_share)[None]
    new_up = (momentum_decay * up_momentum[0] + up_share)[None]
    new_down = (momentum_decay * down_momentum[0] + down_share)[None]
    return (backs[None], new_gate, new_up, new_down)


def masks_even(count):
    return sorted(range(2, count, 2), key=lambda m: -(m & -m))


def relay_kernel(
    n,
    depth,
    li_ref,
    cot_ref,
    gate_hbm,
    up_hbm,
    down_hbm,
    back_ref,
    normed_out,
    incoming_out,
    hidden_out,
    gate_out,
    up_out,
    gate_w,
    up_w,
    down_w,
    nrm,
    inc,
    slope,
    silu_s,
    exact_s,
    inv_s,
    parts,
    rs_recv,
    z_send,
    gate_t,
    up_t,
    down_t,
    load_sem,
    ssem,
    rsem,
):
    micro, rows, width = li_ref.shape
    hid = down_w.shape[0]
    total = n * rows
    half = width // 2
    bits = n.bit_length() - 1
    pieces = ssem.shape[1]
    size = rows // pieces
    s = lax.axis_index("segment")
    t = lax.axis_index("tp")
    p = lax.div(s, 2)
    d = lax.rem(s, 2)
    mirror = s + 1 - 2 * d

    def flip(mask):
        value = t
        for b in range(bits):
            if mask >> b & 1:
                value = value + (1 << b) * (1 - 2 * lax.rem(lax.div(t, 1 << b), 2))
        return value

    def piece(c):
        return pl.ds(c * size, size)

    def copy(k, c, kind, slot, src, dst, device):
        return pltpu.make_async_remote_copy(
            src_ref=src,
            dst_ref=dst,
            send_sem=ssem.at[k, c, kind * n + slot],
            recv_sem=rsem.at[k, c, kind * n + slot],
            device_id=device,
            device_id_type=pl.DeviceIdType.MESH,
        )

    loads = [
        pltpu.make_async_copy(a, b, load_sem.at[i])
        for i, (a, b) in enumerate(((gate_hbm, gate_w), (up_hbm, up_w), (down_hbm, down_w)))
    ]
    for load in loads:
        load.start()

    barrier = pltpu.get_barrier_semaphore()

    def greet(device):
        pl.semaphore_signal(
            barrier, inc=1, device_id=device, device_id_type=pl.DeviceIdType.MESH
        )

    for b in range(bits):
        greet({"tp": flip(1 << b)})
    greet({"segment": mirror})

    @pl.when(p > 0)
    def _():
        greet({"segment": s - 2})

    @pl.when(p < depth - 1)
    def _():
        greet({"segment": s + 2})

    for k in range(micro):
        x = li_ref[k].astype(jnp.float32)
        inv = lax.rsqrt(jnp.mean(x * x, axis=-1, keepdims=True) + epsilon)
        exact = x * inv
        inv_s[k] = inv
        exact_s[k] = exact
        nrm[0, k, t] = exact.astype(jnp.bfloat16)

    peers = bits + 1 + jnp.minimum(p, 1) + jnp.minimum(depth - 1 - p, 1)
    pl.semaphore_wait(barrier, peers)

    def ag_copy(kind, k, c, m, b):
        buf = (nrm, inc)[kind]
        block = buf.at[0, k, flip(m), piece(c)]
        return copy(k, c, kind, m | 1 << b, block, block, {"tp": flip(1 << b)})

    def ag_arrival(kind, k, c, slot):
        buf = (nrm, inc)[kind]
        block = buf.at[0, k, flip(slot), piece(c)]
        low = slot & -slot
        return copy(k, c, kind, slot, block, block, {"tp": flip(low)})

    def ag_start(kind, k, c):
        for b in reversed(range(bits)):
            ag_copy(kind, k, c, 0, b).start()

    def ag_forward(kind, k):
        for c in range(pieces):
            for m in masks_even(n):
                ag_arrival(kind, k, c, m).wait_recv()
                for b in reversed(range(bits)):
                    if 1 << b < (m & -m):
                        ag_copy(kind, k, c, m, b).start()
                if c == pieces - 1:
                    mirror_copy(kind, k, m).start()

    def ag_finish(kind, k):
        for c in range(pieces):
            for m in range(1, n, 2):
                ag_arrival(kind, k, c, m).wait_recv()

    def mirror_copy(kind, k, m):
        buf = (nrm, inc)[kind]
        block = flip(m)
        return copy(
            k, 0, 3 + kind, m, buf.at[0, k, block], buf.at[1, k, block], {"segment": mirror}
        )

    def pass_copy(kind, k, m, arriving=0):
        block = (nrm, inc)[kind].at[1, k, flip(m | arriving)]
        return copy(k, 0, 5 + kind, m, block, block, {"tp": flip(1)})

    def mirror_pass(kind, k):
        for m in range(0, n, 2):
            mirror_copy(kind, k, m).wait_recv()
            pass_copy(kind, k, m).start()

    def mirror_wait(kind, k):
        for m in range(0, n, 2):
            pass_copy(kind, k, m, 1).wait_recv()

    def forward(side, k):
        start = (side * micro + k) * total
        lhs = nrm[side, k].reshape(total, width)
        step = min(256, hid)

        @pl.loop(0, hid // step)
        def _(j):
            cols = pl.ds(pl.multiple_of(j * step, step), step)
            g = jnp.dot(lhs, gate_w[:, cols], preferred_element_type=jnp.float32)
            u = jnp.dot(lhs, up_w[:, cols], preferred_element_type=jnp.float32)
            sigma = jax.nn.sigmoid(g)
            sl = g * sigma
            hidden_out[start : start + total, cols] = (sl * u).astype(jnp.bfloat16)
            slope[start : start + total, cols] = u * sigma * (1.0 + g * (1.0 - sigma))
            silu_s[start : start + total, cols] = sl

        keep = pl.ds(pl.multiple_of(d * half, half), half)
        normed_out[start : start + total, :] = nrm[side, k, :, :, keep].reshape(total, half)

    def factors(side, k, turned):
        start = (side * micro + k) * total
        lhs = inc[side, k].reshape(total, width)
        step = min(512, hid)

        @pl.loop(0, hid // step)
        def _(j):
            cols = pl.ds(pl.multiple_of(j * step, step), step)
            if turned:
                grad = jnp.dot(lhs, down_t[:, cols], preferred_element_type=jnp.float32)
            else:
                grad = contract_last(lhs, down_w[cols, :])
            gate_out[start : start + total, cols] = (
                grad * slope[start : start + total, cols]
            ).astype(jnp.bfloat16)
            up_out[start : start + total, cols] = (
                grad * silu_s[start : start + total, cols]
            ).astype(jnp.bfloat16)

    def keep_incoming(side, k):
        start = (side * micro + k) * total
        keep = pl.ds(pl.multiple_of(d * half, half), half)
        incoming_out[start : start + total, :] = inc[side, k, :, :, keep].reshape(total, half)

    def partial_grads(k, turned):
        start = k * total
        step = min(512, width)

        @pl.loop(0, width // step)
        def _(j):
            gg = gate_out[start : start + total, :]
            ug = up_out[start : start + total, :]
            cols = pl.ds(pl.multiple_of(j * step, step), step)
            if turned:
                part = jnp.dot(gg, gate_t[:, cols], preferred_element_type=jnp.float32)
                part = part + jnp.dot(ug, up_t[:, cols], preferred_element_type=jnp.float32)
            else:
                part = contract_last(gg, gate_w[cols, :]) + contract_last(ug, up_w[cols, :])
            parts[k, :, :, cols] = part.astype(jnp.bfloat16).reshape(n, rows, step)

    def turn(source, target):
        step = 256

        @pl.loop(0, source.shape[1] // step)
        def _(j):
            cols = pl.ds(pl.multiple_of(j * step, step), step)
            target[cols, :] = source[:, cols].T

    def rs_copy(k, c, b, m):
        q = m | 1 << b
        src = parts.at[k, flip(q), piece(c)]
        return copy(k, c, 2, q, src, rs_recv.at[k, q, piece(c)], {"tp": flip(1 << b)})

    def rs_round(k, c, b):
        for m in range(0, n, 1 << (b + 1)):
            q = m | 1 << b
            if b:
                value = parts[k, flip(q), piece(c)].astype(jnp.float32)
                for lower in range(b):
                    value = value + rs_recv[k, q | 1 << lower, piece(c)].astype(jnp.float32)
                parts[k, flip(q), piece(c)] = value.astype(jnp.bfloat16)
            rs_copy(k, c, b, m).start()

    def rs_wait(k, c, b):
        for m in range(0, n, 1 << (b + 1)):
            rs_copy(k, c, b, m).wait_recv()

    def z_copy(k, c, step=2):
        dst = inc.at[0, k, t, piece(c)]
        return copy(k, c, 2, 0, z_send.at[k, piece(c)], dst, {"segment": s + step})

    def finish(k, c):
        span = piece(c)
        value = parts[k, t, span].astype(jnp.float32)
        for b in range(bits):
            value = value + rs_recv[k, 1 << b, span].astype(jnp.float32)
        base = exact_s[k, span]
        back = inc[0, k, t, span].astype(jnp.float32) + inv_s[k, span] * (
            value - base * jnp.mean(value * base, axis=-1, keepdims=True)
        )
        back = back.astype(jnp.bfloat16)
        z_send[k, span] = back

        @pl.when(p < depth - 1)
        def _():
            z_copy(k, c).start()

        back_ref[k, span] = back

    first = p == 0
    early = jnp.logical_and(p > 0, p * 2 >= depth)

    def open_rows(k):
        for c in range(pieces):
            ag_start(0, k, c)

        @pl.when(first)
        def _():
            inc[0, k, t] = cot_ref[d, k]
            for c in range(pieces):
                ag_start(1, k, c)

        mirror_copy(0, k, 0).start()

        @pl.when(first)
        def _():
            mirror_copy(1, k, 0).start()

    def spread(k):
        ag_forward(0, k)

        @pl.when(first)
        def _():
            ag_forward(1, k)

        ag_finish(0, k)

    def mirror_forward():
        for k in range(micro):
            mirror_pass(0, k)
        for k in range(micro):
            mirror_wait(0, k)
            forward(1, k)

    for k in range(micro):
        open_rows(k)
    spread(0)
    loads[0].wait()
    loads[1].wait()
    forward(0, 0)
    loads[2].wait()

    @pl.when(jnp.logical_not(first))
    def _():
        for k in range(1, micro):
            spread(k)
            forward(0, k)
        turn(down_w, down_t)
        turn(gate_w, gate_t)
        turn(up_w, up_t)

    @pl.when(early)
    def _():
        mirror_forward()

    def receive(k):
        @pl.when(jnp.logical_not(first))
        def _():
            for c in range(pieces):
                z_copy(k, c, -2).wait_recv()
                ag_start(1, k, c)
            mirror_copy(1, k, 0).start()

    def relay(k):
        @pl.when(jnp.logical_not(first))
        def _():
            ag_forward(1, k)

    def compute(k):
        ag_finish(1, k)

        @pl.when(first)
        def _():
            factors(0, k, False)
            partial_grads(k, False)

        @pl.when(jnp.logical_not(first))
        def _():
            factors(0, k, True)
            partial_grads(k, True)

        for c in range(pieces):
            rs_round(k, c, 0)
        keep_incoming(0, k)

    def reduce(k):
        for b in range(1, bits):
            for c in range(pieces):
                rs_wait(k, c, b - 1)
                rs_round(k, c, b)

    def end(k):
        for c in range(pieces):
            rs_wait(k, c, bits - 1)
            finish(k, c)

    def mirror_factors(k, turned):
        mirror_wait(1, k)
        factors(1, k, turned)
        keep_incoming(1, k)

    receive(0)
    relay(0)
    compute(0)

    @pl.when(first)
    def _():
        for k in range(1, micro):
            spread(k)
            forward(0, k)

    for k in range(1, micro):
        reduce(k - 1)
        receive(k)
        relay(k)
        end(k - 1)
        mirror_pass(1, k - 1)
        compute(k)
    reduce(micro - 1)
    mirror_pass(1, micro - 1)

    @pl.when(early)
    def _():
        for k in range(micro - 1):
            mirror_factors(k, True)

    @pl.when(jnp.logical_and(early, p == depth - 1))
    def _():
        mirror_factors(micro - 1, True)

    end(micro - 1)

    @pl.when(jnp.logical_and(early, p < depth - 1))
    def _():
        mirror_factors(micro - 1, True)

    @pl.when(jnp.logical_not(early))
    def _():
        mirror_forward()
        for k in range(micro):
            mirror_factors(k, False)

    for k in range(micro):
        for kind in range(2):
            for m in range(0, n, 2):
                mirror_copy(kind, k, m).wait_send()
                pass_copy(kind, k, m).wait_send()
        for c in range(pieces):
            for b in range(bits):
                for m in range(0, n, 1 << (b + 1)):
                    for kind in range(2):
                        ag_copy(kind, k, c, m, b).wait_send()
                    rs_copy(k, c, b, m).wait_send()

            @pl.when(p < depth - 1)
            def _():
                z_copy(k, c).wait_send()


def relayed(
    segments,
    n,
    layer_inputs,
    cotangent,
    gate_weight,
    up_weight,
    down_weight,
    gate_momentum,
    up_momentum,
    down_momentum,
):
    _, micro, rows, width = layer_inputs.shape
    hid = gate_weight.shape[2]
    half = width // 2
    flat = 2 * micro * n * rows
    vmem = pl.BlockSpec(memory_space=pltpu.VMEM)
    hbm = pl.BlockSpec(memory_space=pl.ANY)
    pieces = 2 if rows % 32 == 0 else 1
    bf, f32 = jnp.bfloat16, jnp.float32
    back, normed, incoming, hidden, gate, up = pl.pallas_call(
        functools.partial(relay_kernel, n, segments // 2),
        name="relay",
        out_shape=(
            jax.ShapeDtypeStruct((micro, rows, width), bf),
            jax.ShapeDtypeStruct((flat, half), bf),
            jax.ShapeDtypeStruct((flat, half), bf),
            jax.ShapeDtypeStruct((flat, hid), bf),
            jax.ShapeDtypeStruct((flat, hid), bf),
            jax.ShapeDtypeStruct((flat, hid), bf),
        ),
        in_specs=[vmem, vmem, hbm, hbm, hbm],
        out_specs=(vmem,) * 6,
        scratch_shapes=[
            pltpu.VMEM((width, hid), bf),
            pltpu.VMEM((width, hid), bf),
            pltpu.VMEM((hid, width), bf),
            pltpu.VMEM((2, micro, n, rows, width), bf),
            pltpu.VMEM((2, micro, n, rows, width), bf),
            pltpu.VMEM((flat, hid), f32),
            pltpu.VMEM((flat, hid), f32),
            pltpu.VMEM((micro, rows, width), f32),
            pltpu.VMEM((micro, rows, 1), f32),
            pltpu.VMEM((micro, n, rows, width), bf),
            pltpu.VMEM((micro, n, rows, width), bf),
            pltpu.VMEM((micro, rows, width), bf),
            pltpu.VMEM((hid, width), bf),
            pltpu.VMEM((hid, width), bf),
            pltpu.VMEM((width, hid), bf),
            pltpu.SemaphoreType.DMA((3,)),
            pltpu.SemaphoreType.DMA((micro, pieces, 7 * n)),
            pltpu.SemaphoreType.DMA((micro, pieces, 7 * n)),
        ],
        compiler_params=pltpu.CompilerParams(
            collective_id=0, has_side_effects=True, vmem_limit_bytes=60 << 20
        ),
    )(layer_inputs[0], cotangent, gate_weight[0], up_weight[0], down_weight[0])
    new_gate = momentum_decay * gate_momentum[0] + contract_rows(normed, gate)
    new_up = momentum_decay * up_momentum[0] + contract_rows(normed, up)
    new_down = momentum_decay * down_momentum[0] + contract_rows(hidden, incoming)
    return (back[None], new_gate[None], new_up[None], new_down[None])


def choose(segments, n, *arrays):
    rows = arrays[0].shape[2]
    if rows % 16 == 0 and n > 1 and n & (n - 1) == 0:
        return relayed(segments, n, *arrays)
    return shards(*arrays)


def solution(mesh):
    body = functools.partial(choose, mesh.shape["segment"], mesh.shape["tp"])
    return jax.shard_map(
        body,
        mesh=mesh,
        in_specs=(
            P("segment", None, "tp", None),
            P(None, None, "tp", None),
            P("segment", None, "tp"),
            P("segment", None, "tp"),
            P("segment", "tp", None),
            P("segment", None, "tp"),
            P("segment", None, "tp"),
            P("segment", "tp", None),
        ),
        out_specs=(
            P("segment", None, "tp", None),
            P("segment", None, "tp"),
            P("segment", None, "tp"),
            P("segment", "tp", None),
        ),
        check_vma=False,
    )
```

```python
import functools
import jax
import jax.numpy as jnp
from jax import lax
from jax.experimental import pallas as pl
from jax.experimental.pallas import tpu as pltpu
from jax.sharding import PartitionSpec as P

epsilon = 1e-05
momentum_decay = 0.9


def passed_along(block, axis, distance):
    devices = range(lax.axis_size(axis))
    route = [(i - distance, i) for i in devices if i - distance in devices]
    return lax.ppermute(block, axis, route)


def partner(block, axis, distance):
    count = lax.axis_size(axis)
    route = []
    for low in range(count):
        high = low | 1 << distance
        if high != low and high < count:
            route += [(low, high), (high, low)]
    return lax.ppermute(block, axis, route)


def contract_last(left, right):
    return lax.dot_general(
        left, right, (((1,), (1,)), ((), ())), preferred_element_type=jnp.float32
    )


def contract_rows(left, right):
    return lax.dot_general(
        left, right, (((0,), (0,)), ((), ())), preferred_element_type=jnp.float32
    )


def rounded(values):
    return lax.optimization_barrier(values.astype(jnp.bfloat16)).astype(jnp.float32)


def project(rows, gate_w, up_w):
    gate = jnp.dot(rows, gate_w, preferred_element_type=jnp.float32)
    up = jnp.dot(rows, up_w, preferred_element_type=jnp.float32)
    return (gate, up)


def backward_factors(incoming_rows, gate, up, down_w):
    hidden_grad = contract_last(incoming_rows, down_w)
    sigma = jax.nn.sigmoid(gate)
    silu = gate * sigma
    hidden = (silu * up).astype(jnp.bfloat16)
    gate_grad = (hidden_grad * up * sigma * (1.0 + gate * (1.0 - sigma))).astype(jnp.bfloat16)
    up_grad = (hidden_grad * silu).astype(jnp.bfloat16)
    return (hidden, gate_grad, up_grad)


def owned(array, start, size, axis):
    return lax.dynamic_slice_in_dim(array, start, size, axis)


def shards(
    layer_inputs,
    cotangent,
    gate_weight,
    up_weight,
    down_weight,
    gate_momentum,
    up_momentum,
    down_momentum,
):
    segments = lax.axis_size("segment")
    depth = segments // 2
    segment = lax.axis_index("segment")
    direction = segment % 2
    lower = direction == 0
    position = segment // 2
    gate_w = gate_weight[0]
    up_w = up_weight[0]
    down_w = down_weight[0]
    inputs = layer_inputs[0].astype(jnp.float32)
    micro, rows_dev, width = inputs.shape
    half = width // 2
    hidden_dev = gate_w.shape[1]
    total_rows = rows_dev * lax.axis_size("tp")
    inverse_norm = lax.rsqrt(jnp.mean(inputs * inputs, axis=-1, keepdims=True) + epsilon)
    exact = inputs * inverse_norm
    normed = exact.astype(jnp.bfloat16)
    entry = lax.dynamic_index_in_dim(cotangent, direction, 0, keepdims=False)
    ticks = depth + micro - 1
    wide_store = jnp.zeros((micro, total_rows, width), jnp.bfloat16)
    narrow_store = jnp.zeros((micro, total_rows, hidden_dev), jnp.bfloat16)
    extra = (wide_store, narrow_store, narrow_store, narrow_store) + (wide_store,)

    def process(tick, received, state):
        outgoing, backs, extra = state
        index = tick - position
        active = (index >= 0) & (index < micro)
        slot = jnp.clip(index, 0, micro - 1)
        local_in = jnp.where(position == 0, entry[slot], received)
        incoming_rows = lax.all_gather(local_in, "tp", axis=0, tiled=True)
        full_rows = lax.all_gather(normed[slot], "tp", axis=0, tiled=True)

        def factors():
            gate, up = project(full_rows, gate_w, up_w)
            return backward_factors(incoming_rows, gate, up, down_w)

        def resting():
            blank = jnp.zeros((total_rows, hidden_dev), jnp.bfloat16)
            return (blank, blank, blank)

        hidden, gate_grad, up_grad = lax.cond(active, factors, resting)
        count = lax.axis_size("tp") * rows_dev

        def compute():
            return contract_last(gate_grad, gate_w) + contract_last(up_grad, up_w)

        def quiet():
            return jnp.zeros((count, width), jnp.float32)

        normed_grad = lax.psum_scatter(
            lax.cond(active, compute, quiet).astype(jnp.bfloat16),
            "tp",
            scatter_dimension=0,
            tiled=True,
        ).astype(jnp.float32)
        scale = inverse_norm[slot]
        base = exact[slot]
        back = local_in.astype(jnp.float32) + scale * (
            normed_grad - base * jnp.mean(normed_grad * base, axis=-1, keepdims=True)
        )
        back = back.astype(jnp.bfloat16)
        backs = lax.dynamic_update_index_in_dim(
            backs, jnp.where(active, back, backs[slot]), slot, 0
        )
        fresh = (incoming_rows, hidden, gate_grad, up_grad) + (full_rows,)
        extra = tuple(
            (
                lax.dynamic_update_index_in_dim(
                    store, jnp.where(active, item, store[slot]), slot, 0
                )
                for store, item in zip(extra, fresh)
            )
        )
        return (back, backs, extra)

    zero_rows = jnp.zeros((rows_dev, width), jnp.bfloat16)
    state = process(
        0, zero_rows, (zero_rows, jnp.zeros((micro, rows_dev, width), jnp.bfloat16), extra)
    )

    def advance(tick, state):
        received = passed_along(state[0], "segment", 2)
        return process(tick, received, state)

    outgoing, backs, extra = lax.fori_loop(1, ticks, advance, state)
    keep_start = jnp.where(lower, 0, half)
    send_start = half - keep_start
    flat_rows = micro * total_rows
    normed_all = extra[4]
    normed_flat = normed_all.reshape(flat_rows, width)
    incoming_flat = extra[0].reshape(flat_rows, width)
    hidden_flat = extra[1].reshape(flat_rows, hidden_dev)
    gate_flat = extra[2].reshape(flat_rows, hidden_dev)
    up_flat = extra[3].reshape(flat_rows, hidden_dev)
    arrived = partner(
        (
            owned(normed_flat, send_start, half, 1),
            owned(incoming_flat, send_start, half, 1),
            hidden_flat,
            gate_flat,
            up_flat,
        ),
        "segment",
        0,
    )
    normed_keep = owned(normed_flat, keep_start, half, 1)
    incoming_keep = owned(incoming_flat, keep_start, half, 1)
    gate_share = contract_rows(normed_keep, gate_flat) + rounded(
        contract_rows(arrived[0], arrived[3])
    )
    up_share = contract_rows(normed_keep, up_flat) + rounded(contract_rows(arrived[0], arrived[4]))
    down_share = contract_rows(hidden_flat, incoming_keep) + rounded(
        contract_rows(arrived[2], arrived[1])
    )
    new_gate = (momentum_decay * gate_momentum[0] + gate_share)[None]
    new_up = (momentum_decay * up_momentum[0] + up_share)[None]
    new_down = (momentum_decay * down_momentum[0] + down_share)[None]
    return (backs[None], new_gate, new_up, new_down)


def masks_even(count):
    return sorted(range(2, count, 2), key=lambda m: -(m & -m))


def relay_kernel(
    n,
    depth,
    li_ref,
    cot_ref,
    gate_hbm,
    up_hbm,
    down_hbm,
    back_ref,
    normed_out,
    incoming_out,
    hidden_out,
    gate_out,
    up_out,
    gate_w,
    up_w,
    down_w,
    nrm,
    inc,
    slope,
    silu_s,
    exact_s,
    inv_s,
    parts,
    rs_recv,
    z_send,
    gate_t,
    up_t,
    down_t,
    load_sem,
    ssem,
    rsem,
):
    micro, rows, width = li_ref.shape
    hid = down_w.shape[0]
    total = n * rows
    half = width // 2
    bits = n.bit_length() - 1
    pieces = ssem.shape[1]
    size = rows // pieces
    s = lax.axis_index("segment")
    t = lax.axis_index("tp")
    p = lax.div(s, 2)
    d = lax.rem(s, 2)
    mirror = s + 1 - 2 * d

    def flip(mask):
        value = t
        for b in range(bits):
            if mask >> b & 1:
                value = value + (1 << b) * (1 - 2 * lax.rem(lax.div(t, 1 << b), 2))
        return value

    def piece(c):
        return pl.ds(c * size, size)

    def copy(k, c, kind, slot, src, dst, device):
        return pltpu.make_async_remote_copy(
            src_ref=src,
            dst_ref=dst,
            send_sem=ssem.at[k, c, kind * n + slot],
            recv_sem=rsem.at[k, c, kind * n + slot],
            device_id=device,
            device_id_type=pl.DeviceIdType.MESH,
        )

    loads = [
        pltpu.make_async_copy(a, b, load_sem.at[i])
        for i, (a, b) in enumerate(((gate_hbm, gate_w), (up_hbm, up_w), (down_hbm, down_w)))
    ]
    for load in loads:
        load.start()

    barrier = pltpu.get_barrier_semaphore()

    def greet(device):
        pl.semaphore_signal(
            barrier, inc=1, device_id=device, device_id_type=pl.DeviceIdType.MESH
        )

    for b in range(bits):
        greet({"tp": flip(1 << b)})
    greet({"segment": mirror})

    @pl.when(p > 0)
    def _():
        greet({"segment": s - 2})

    @pl.when(p < depth - 1)
    def _():
        greet({"segment": s + 2})

    for k in range(micro):
        x = li_ref[k].astype(jnp.float32)
        inv = lax.rsqrt(jnp.mean(x * x, axis=-1, keepdims=True) + epsilon)
        exact = x * inv
        inv_s[k] = inv
        exact_s[k] = exact
        nrm[0, k, t] = exact.astype(jnp.bfloat16)

    peers = bits + 1 + jnp.minimum(p, 1) + jnp.minimum(depth - 1 - p, 1)
    pl.semaphore_wait(barrier, peers)

    def ag_copy(kind, k, c, m, b):
        buf = (nrm, inc)[kind]
        block = buf.at[0, k, flip(m), piece(c)]
        return copy(k, c, kind, m | 1 << b, block, block, {"tp": flip(1 << b)})

    def ag_arrival(kind, k, c, slot):
        buf = (nrm, inc)[kind]
        block = buf.at[0, k, flip(slot), piece(c)]
        low = slot & -slot
        return copy(k, c, kind, slot, block, block, {"tp": flip(low)})

    def ag_start(kind, k, c):
        for b in reversed(range(bits)):
            ag_copy(kind, k, c, 0, b).start()

    def ag_forward(kind, k):
        for c in range(pieces):
            for m in masks_even(n):
                ag_arrival(kind, k, c, m).wait_recv()
                for b in reversed(range(bits)):
                    if 1 << b < (m & -m):
                        ag_copy(kind, k, c, m, b).start()
                if c == pieces - 1:
                    mirror_copy(kind, k, m).start()

    def ag_finish(kind, k):
        for c in range(pieces):
            for m in range(1, n, 2):
                ag_arrival(kind, k, c, m).wait_recv()

    def mirror_copy(kind, k, m):
        buf = (nrm, inc)[kind]
        block = flip(m)
        return copy(
            k, 0, 3 + kind, m, buf.at[0, k, block], buf.at[1, k, block], {"segment": mirror}
        )

    def pass_copy(kind, k, m, arriving=0):
        block = (nrm, inc)[kind].at[1, k, flip(m | arriving)]
        return copy(k, 0, 5 + kind, m, block, block, {"tp": flip(1)})

    def mirror_pass(kind, k):
        for m in range(0, n, 2):
            mirror_copy(kind, k, m).wait_recv()
            pass_copy(kind, k, m).start()

    def mirror_wait(kind, k):
        for m in range(0, n, 2):
            pass_copy(kind, k, m, 1).wait_recv()

    def forward(side, k):
        start = (side * micro + k) * total
        lhs = nrm[side, k].reshape(total, width)
        step = min(256, hid)

        @pl.loop(0, hid // step)
        def _(j):
            cols = pl.ds(pl.multiple_of(j * step, step), step)
            g = jnp.dot(lhs, gate_w[:, cols], preferred_element_type=jnp.float32)
            u = jnp.dot(lhs, up_w[:, cols], preferred_element_type=jnp.float32)
            sigma = jax.nn.sigmoid(g)
            sl = g * sigma
            hidden_out[start : start + total, cols] = (sl * u).astype(jnp.bfloat16)
            slope[start : start + total, cols] = u * sigma * (1.0 + g * (1.0 - sigma))
            silu_s[start : start + total, cols] = sl

        keep = pl.ds(pl.multiple_of(d * half, half), half)
        normed_out[start : start + total, :] = nrm[side, k, :, :, keep].reshape(total, half)

    def factors(side, k, turned):
        start = (side * micro + k) * total
        lhs = inc[side, k].reshape(total, width)
        step = min(1024, hid)

        @pl.loop(0, hid // step)
        def _(j):
            cols = pl.ds(pl.multiple_of(j * step, step), step)
            if turned:
                grad = jnp.dot(lhs, down_t[:, cols], preferred_element_type=jnp.float32)
            else:
                grad = contract_last(lhs, down_w[cols, :])
            gate_out[start : start + total, cols] = (
                grad * slope[start : start + total, cols]
            ).astype(jnp.bfloat16)
            up_out[start : start + total, cols] = (
                grad * silu_s[start : start + total, cols]
            ).astype(jnp.bfloat16)

    def keep_incoming(side, k):
        start = (side * micro + k) * total
        keep = pl.ds(pl.multiple_of(d * half, half), half)
        incoming_out[start : start + total, :] = inc[side, k, :, :, keep].reshape(total, half)

    def partial_grads(k, turned):
        start = k * total
        step = min(1024, width)

        @pl.loop(0, width // step)
        def _(j):
            gg = gate_out[start : start + total, :]
            ug = up_out[start : start + total, :]
            cols = pl.ds(pl.multiple_of(j * step, step), step)
            if turned:
                part = jnp.dot(gg, gate_t[:, cols], preferred_element_type=jnp.float32)
                part = part + jnp.dot(ug, up_t[:, cols], preferred_element_type=jnp.float32)
            else:
                part = contract_last(gg, gate_w[cols, :]) + contract_last(ug, up_w[cols, :])
            parts[k, :, :, cols] = part.astype(jnp.bfloat16).reshape(n, rows, step)

    def turn(source, target):
        step = 256

        @pl.loop(0, source.shape[1] // step)
        def _(j):
            cols = pl.ds(pl.multiple_of(j * step, step), step)
            target[cols, :] = source[:, cols].T

    def rs_copy(k, c, b, m):
        q = m | 1 << b
        src = parts.at[k, flip(q), piece(c)]
        return copy(k, c, 2, q, src, rs_recv.at[k, q, piece(c)], {"tp": flip(1 << b)})

    def rs_round(k, c, b):
        for m in range(0, n, 1 << (b + 1)):
            q = m | 1 << b
            if b:
                value = parts[k, flip(q), piece(c)].astype(jnp.float32)
                for lower in range(b):
                    value = value + rs_recv[k, q | 1 << lower, piece(c)].astype(jnp.float32)
                parts[k, flip(q), piece(c)] = value.astype(jnp.bfloat16)
            rs_copy(k, c, b, m).start()

    def rs_wait(k, c, b):
        for m in range(0, n, 1 << (b + 1)):
            rs_copy(k, c, b, m).wait_recv()

    def z_copy(k, c, step=2):
        dst = inc.at[0, k, t, piece(c)]
        return copy(k, c, 2, 0, z_send.at[k, piece(c)], dst, {"segment": s + step})

    def finish(k, c):
        span = piece(c)
        value = parts[k, t, span].astype(jnp.float32)
        for b in range(bits):
            value = value + rs_recv[k, 1 << b, span].astype(jnp.float32)
        base = exact_s[k, span]
        back = inc[0, k, t, span].astype(jnp.float32) + inv_s[k, span] * (
            value - base * jnp.mean(value * base, axis=-1, keepdims=True)
        )
        back = back.astype(jnp.bfloat16)
        z_send[k, span] = back

        @pl.when(p < depth - 1)
        def _():
            z_copy(k, c).start()

        back_ref[k, span] = back

    first = p == 0
    early = jnp.logical_and(p > 0, p * 2 >= depth)

    def open_rows(k):
        for c in range(pieces):
            ag_start(0, k, c)

        @pl.when(first)
        def _():
            inc[0, k, t] = cot_ref[d, k]
            for c in range(pieces):
                ag_start(1, k, c)

        mirror_copy(0, k, 0).start()

        @pl.when(first)
        def _():
            mirror_copy(1, k, 0).start()

    def spread(k):
        ag_forward(0, k)

        @pl.when(first)
        def _():
            ag_forward(1, k)

        ag_finish(0, k)

    def mirror_forward():
        for k in range(micro):
            mirror_pass(0, k)
        for k in range(micro):
            mirror_wait(0, k)
            forward(1, k)

    for k in range(micro):
        open_rows(k)
    spread(0)
    loads[0].wait()
    loads[1].wait()
    forward(0, 0)
    loads[2].wait()

    @pl.when(jnp.logical_not(first))
    def _():
        for k in range(1, micro):
            spread(k)
            forward(0, k)
        turn(down_w, down_t)
        turn(gate_w, gate_t)
        turn(up_w, up_t)

    @pl.when(early)
    def _():
        mirror_forward()

    def receive(k):
        @pl.when(jnp.logical_not(first))
        def _():
            for c in range(pieces):
                z_copy(k, c, -2).wait_recv()
                ag_start(1, k, c)
            mirror_copy(1, k, 0).start()

    def relay(k):
        @pl.when(jnp.logical_not(first))
        def _():
            ag_forward(1, k)

    def compute(k):
        ag_finish(1, k)

        @pl.when(first)
        def _():
            factors(0, k, False)
            partial_grads(k, False)

        @pl.when(jnp.logical_not(first))
        def _():
            factors(0, k, True)
            partial_grads(k, True)

        for c in range(pieces):
            rs_round(k, c, 0)
        keep_incoming(0, k)

    def reduce(k):
        for b in range(1, bits):
            for c in range(pieces):
                rs_wait(k, c, b - 1)
                rs_round(k, c, b)

    def end(k):
        for c in range(pieces):
            rs_wait(k, c, bits - 1)
            finish(k, c)

    def mirror_factors(k, turned):
        mirror_wait(1, k)
        factors(1, k, turned)
        keep_incoming(1, k)

    receive(0)
    relay(0)
    compute(0)

    for k in range(1, micro):
        reduce(k - 1)

        @pl.when(first)
        def _():
            spread(k)
            forward(0, k)

        receive(k)
        relay(k)
        end(k - 1)
        mirror_pass(1, k - 1)
        compute(k)
    reduce(micro - 1)
    mirror_pass(1, micro - 1)

    @pl.when(early)
    def _():
        for k in range(micro - 1):
            mirror_factors(k, True)

    @pl.when(jnp.logical_and(early, p == depth - 1))
    def _():
        mirror_factors(micro - 1, True)

    end(micro - 1)

    @pl.when(jnp.logical_and(early, p < depth - 1))
    def _():
        mirror_factors(micro - 1, True)

    @pl.when(jnp.logical_not(early))
    def _():
        mirror_forward()
        for k in range(micro):
            mirror_factors(k, False)

    for k in range(micro):
        for kind in range(2):
            for m in range(0, n, 2):
                mirror_copy(kind, k, m).wait_send()
                pass_copy(kind, k, m).wait_send()
        for c in range(pieces):
            for b in range(bits):
                for m in range(0, n, 1 << (b + 1)):
                    for kind in range(2):
                        ag_copy(kind, k, c, m, b).wait_send()
                    rs_copy(k, c, b, m).wait_send()

            @pl.when(p < depth - 1)
            def _():
                z_copy(k, c).wait_send()


def relayed(
    segments,
    n,
    layer_inputs,
    cotangent,
    gate_weight,
    up_weight,
    down_weight,
    gate_momentum,
    up_momentum,
    down_momentum,
):
    _, micro, rows, width = layer_inputs.shape
    hid = gate_weight.shape[2]
    half = width // 2
    flat = 2 * micro * n * rows
    vmem = pl.BlockSpec(memory_space=pltpu.VMEM)
    hbm = pl.BlockSpec(memory_space=pl.ANY)
    pieces = 2 if rows % 32 == 0 else 1
    bf, f32 = jnp.bfloat16, jnp.float32
    back, normed, incoming, hidden, gate, up = pl.pallas_call(
        functools.partial(relay_kernel, n, segments // 2),
        name="relay",
        out_shape=(
            jax.ShapeDtypeStruct((micro, rows, width), bf),
            jax.ShapeDtypeStruct((flat, half), bf),
            jax.ShapeDtypeStruct((flat, half), bf),
            jax.ShapeDtypeStruct((flat, hid), bf),
            jax.ShapeDtypeStruct((flat, hid), bf),
            jax.ShapeDtypeStruct((flat, hid), bf),
        ),
        in_specs=[vmem, vmem, hbm, hbm, hbm],
        out_specs=(vmem,) * 6,
        scratch_shapes=[
            pltpu.VMEM((width, hid), bf),
            pltpu.VMEM((width, hid), bf),
            pltpu.VMEM((hid, width), bf),
            pltpu.VMEM((2, micro, n, rows, width), bf),
            pltpu.VMEM((2, micro, n, rows, width), bf),
            pltpu.VMEM((flat, hid), f32),
            pltpu.VMEM((flat, hid), f32),
            pltpu.VMEM((micro, rows, width), f32),
            pltpu.VMEM((micro, rows, 1), f32),
            pltpu.VMEM((micro, n, rows, width), bf),
            pltpu.VMEM((micro, n, rows, width), bf),
            pltpu.VMEM((micro, rows, width), bf),
            pltpu.VMEM((hid, width), bf),
            pltpu.VMEM((hid, width), bf),
            pltpu.VMEM((width, hid), bf),
            pltpu.SemaphoreType.DMA((3,)),
            pltpu.SemaphoreType.DMA((micro, pieces, 7 * n)),
            pltpu.SemaphoreType.DMA((micro, pieces, 7 * n)),
        ],
        compiler_params=pltpu.CompilerParams(
            collective_id=0, has_side_effects=True, vmem_limit_bytes=60 << 20
        ),
    )(layer_inputs[0], cotangent, gate_weight[0], up_weight[0], down_weight[0])
    new_gate = momentum_decay * gate_momentum[0] + contract_rows(normed, gate)
    new_up = momentum_decay * up_momentum[0] + contract_rows(normed, up)
    new_down = momentum_decay * down_momentum[0] + contract_rows(hidden, incoming)
    return (back[None], new_gate[None], new_up[None], new_down[None])


def choose(segments, n, *arrays):
    rows = arrays[0].shape[2]
    if rows % 16 == 0 and n > 1 and n & (n - 1) == 0:
        return relayed(segments, n, *arrays)
    return shards(*arrays)


def solution(mesh):
    body = functools.partial(choose, mesh.shape["segment"], mesh.shape["tp"])
    return jax.shard_map(
        body,
        mesh=mesh,
        in_specs=(
            P("segment", None, "tp", None),
            P(None, None, "tp", None),
            P("segment", None, "tp"),
            P("segment", None, "tp"),
            P("segment", "tp", None),
            P("segment", None, "tp"),
            P("segment", None, "tp"),
            P("segment", "tp", None),
        ),
        out_specs=(
            P("segment", None, "tp", None),
            P("segment", None, "tp"),
            P("segment", None, "tp"),
            P("segment", "tp", None),
        ),
        check_vma=False,
    )
```
